32 devices in a mesh: leaf: 8 (over y, x, core), sub: 4 (over z).
Axes of the slice: x: 2, y: 2, z: 4, core: 2. Of those that a mesh axis runs over, the one named last changes fastest.
Arguments:
- charges: float32 [16, 64, 4, 8, 2048], P(None, None, 'sub', 'leaf'), may hold values from -6 to 6
- ordering: int32 [4, 8, 2048], P('sub', 'leaf'), may hold values from 0 to 2047, each once within a row
- jitter: float32 [3, 4, 8, 2048], P(None, 'sub', 'leaf'), may hold values from 0 to 1
- leaf_bases: float32 [4, 8, 64, 2048], P('sub', 'leaf'), may hold values from -0.125 to 0.125
- transfer: float32 [5, 2, 64, 64], replicated, may hold values from -0.5 to 0.5
- coupling: float32 [5, 2, 64, 64], replicated, may hold values from -0.75 to 0.75
Outputs:
- potential: float32 [16, 64, 4, 8, 2048], P(None, None, 'sub', 'leaf')
The draws below stay inside these ranges and needn't reach their ends.
All inputs are finite; a program needn't handle non-finite values.
Results may differ from the reference program's by a relative error of at most 0.0003.
Values sent between devices are 32-bit elements; how exact they have to be, the bound alone decides.
No kernel may reach another device: no remote copies, remote signals or barrier semaphores. Data moves between devices by JAX's collectives and lax.ppermute only.
A program may use at most 128 MiB of HBM per device.

```python
import jax
import jax.numpy as jnp
from jax import lax

VEC = 64
RANK = 64
PTS = 2048
SETS = 16
STRIP = 512
CLUSTERS = 8
SUBTREES = 4
LEVELS = 5


def shard_levels(own_key, shape, shards, smallest, largest):
    gain = 1.0
    for position, parts in shards:
        steps = jax.random.uniform(jax.random.fold_in(jax.random.fold_in(own_key, 6), position), (parts,), jnp.float32, smallest / len(shards), largest / len(shards))
        gain = gain * jnp.repeat(jnp.exp(steps), shape[position] // parts).reshape((-1,) + (1,) * (len(shape) - 1 - position))
    return gain


def scatter_about(rng, dims, width, limit, pieces=(), held_as=jnp.bfloat16):
    entries = jax.random.normal(rng, dims, jnp.float32) * width
    if len(pieces) > 0:
        entries = shard_levels(rng, dims, pieces, -0.22, 0.18) * entries
    return jnp.clip(entries, min=-limit, max=limit).astype(held_as)


def setup_inputs(seed: int = 0) -> dict:
    key_list = jax.random.split(jax.random.key(seed), 7)
    charges = scatter_about(key_list[0], (SETS, VEC, SUBTREES, CLUSTERS, PTS), 1.0, 6.0, ((2, 4), (3, 8)), jnp.float32)
    ordering = jax.vmap(lambda own: jax.random.permutation(own, PTS))(jax.random.split(key_list[1], SUBTREES * CLUSTERS)).reshape((SUBTREES, CLUSTERS, PTS)).astype(jnp.int32)
    jitter = jnp.clip(1.0 * jax.random.uniform(key_list[2], (3, SUBTREES, CLUSTERS, PTS), jnp.float32) ** shard_levels(key_list[2], (3, SUBTREES, CLUSTERS, PTS), ((1, 4), (2, 8)), -0.2, 0.2), 0.0, 1.0)
    leaf_bases = scatter_about(key_list[3], (SUBTREES, CLUSTERS, RANK, PTS), PTS ** -0.5, 0.125, ((0, 4), (1, 8)), jnp.float32)
    transfer = scatter_about(key_list[4], (LEVELS, 2, RANK, RANK), (2 * RANK) ** -0.5, 0.5, (), jnp.float32)
    coupling = scatter_about(key_list[5], (LEVELS, 2, RANK, RANK), RANK ** -0.5, 0.75, (), jnp.float32)
    return dict(charges=charges, ordering=ordering, jitter=jitter, leaf_bases=leaf_bases, transfer=transfer, coupling=coupling)


DELTA_SQ = 0.0025
PRECISE = lax.Precision.HIGHEST

def near_field(src_charges, src_places, tgt_places, near_scale):
    count = tgt_places.shape[1]
    block_rows = min(count, 512)

    def accumulate(step, result):
        first_row = (step * block_rows).astype(jnp.int32)
        targets = lax.dynamic_slice_in_dim(tgt_places, first_row, block_rows, 1)
        distance = jnp.zeros((src_places.shape[1], block_rows), jnp.float32)
        for component in range(3):
            spacing = src_places[component][:, None] - targets[component][None, :]
            distance = distance + spacing * spacing
        weight = near_scale * lax.rsqrt(distance + DELTA_SQ)
        product = jnp.dot(src_charges, weight, precision=PRECISE, preferred_element_type=jnp.float32)
        return lax.dynamic_update_slice_in_dim(result, product, first_row, 1)
    start_value = jnp.zeros((src_charges.shape[0], count), jnp.float32)
    return lax.fori_loop(0, count // block_rows, accumulate, start_value)

def pick_order(block_data, indices):
    return jnp.take(block_data, indices, axis=1)

def reference(charges, ordering, jitter, leaf_bases, transfer, coupling):
    set_count, vector_count = (charges.shape[0], charges.shape[1])
    row_count = set_count * vector_count
    clusters_all = SUBTREES * CLUSTERS
    grouped = charges.reshape(row_count, SUBTREES, CLUSTERS, PTS).transpose(1, 2, 0, 3)
    tree_charges = jax.vmap(jax.vmap(pick_order))(grouped, ordering)
    cluster_ids = jnp.arange(CLUSTERS, dtype=jnp.float32)[None, :, None]
    point_ids = jnp.arange(PTS, dtype=jnp.float32)[None, None, :]
    along_axis = cluster_ids + (point_ids + jitter[0]) / PTS
    places = jnp.stack([along_axis, jitter[1], jitter[2]], axis=2)
    sources = jnp.concatenate([tree_charges, places], axis=2)
    padded = jnp.pad(sources, ((0, 0), (1, 1), (0, 0), (0, 0)))
    near_scale = PTS ** (-0.5)

    def near_one(flat_index):
        sub_index = (flat_index // CLUSTERS).astype(jnp.int32)
        leaf_index = (flat_index % CLUSTERS).astype(jnp.int32)
        zero_index = jnp.zeros((), jnp.int32)
        window = lax.dynamic_slice(padded, (sub_index, leaf_index, zero_index, zero_index), (1, 3, row_count + 3, PTS))[0]
        joined = jnp.concatenate([window[0, :, PTS - STRIP:], window[1], window[2, :, :STRIP]], axis=1)
        return near_field(joined[:row_count], joined[row_count:], window[1, row_count:], near_scale)
    near_all = lax.map(near_one, jnp.arange(clusters_all, dtype=jnp.int32))
    flat_tree = tree_charges.reshape(clusters_all, row_count, PTS)
    flat_bases = leaf_bases.reshape(clusters_all, RANK, PTS)
    moment = jnp.einsum('gsp,grp->gsr', flat_tree, flat_bases, precision=PRECISE)
    moments = [moment]
    for level_index in range(LEVELS):
        current = moments[-1]
        parent = jnp.einsum('nsa,ab->nsb', current[0::2], transfer[level_index, 0], precision=PRECISE)
        parent = parent + jnp.einsum('nsa,ab->nsb', current[1::2], transfer[level_index, 1], precision=PRECISE)
        moments.append(parent)
    expansion = jnp.zeros((1, row_count, RANK), jnp.float32)
    for level_index in reversed(range(LEVELS)):
        current = moments[level_index]
        count = current.shape[0]
        sibling = current.reshape(count // 2, 2, row_count, RANK)[:, ::-1].reshape(count, row_count, RANK)
        inherited = jnp.repeat(expansion, 2, axis=0)
        branch_bits = jnp.arange(count, dtype=jnp.int32) % 2
        couple_mats = coupling[level_index][branch_bits]
        transfer_mats = transfer[level_index][branch_bits]
        expansion = jnp.einsum('nsa,nra->nsr', sibling, couple_mats, precision=PRECISE) + jnp.einsum('nsa,nra->nsr', inherited, transfer_mats, precision=PRECISE)
    far_all = jnp.einsum('gsr,grp->gsp', expansion, flat_bases, precision=PRECISE)
    potential = near_all + far_all
    potential = potential.reshape(SUBTREES, CLUSTERS, set_count, vector_count, PTS).transpose(2, 3, 0, 1, 4)
    return potential
```

```python
import functools
import math

import jax
import jax.numpy as jnp
from jax import lax
from jax.experimental import pallas as pl
from jax.experimental.pallas import tpu as pltpu
from jax.sharding import PartitionSpec as P


DELTA_SQ = 0.0025
PRECISE = lax.Precision.HIGHEST
LANES = 128
ROWS = 256
GROUP = 512
TILE = 256
BF16 = jnp.bfloat16
F32 = jnp.float32
WIDE8 = jnp.float8_e5m2
FINE8 = jnp.float8_e4m3fn
LO_UP = 2.0**20
FULL_UP = 2.0**13
W_UP = 2.0**9
W_LO_UP = 2.0**16
NEAR_DOWN = 2.0**-29
BASE_UP = 2.0**10
MOMENT_DOWN = 2.0**-30


def dot(a, b):
    return jnp.dot(a, b, preferred_element_type=F32)


def split2(value):
    high = value.astype(BF16)
    return high, (value - high.astype(F32)).astype(BF16)


def strip_indices(order_ref, tail, width):
    count = order_ref.shape[1]
    return jnp.where(tail, order_ref[:, count - width :], order_ref[:, :width])


def strip_places(jitter_ref, tail, width, unit):
    count = jitter_ref.shape[2]

    def part(component):
        row = jitter_ref[component]
        return jnp.where(tail, row[:, count - width :], row[:, :width])

    start = jnp.where(tail, count - width, 0)
    index = (lax.broadcasted_iota(jnp.int32, (1, width), 1) + start).astype(F32)
    along = (index + part(0)) * (unit / count)
    return along, part(1) * unit, part(2) * unit


def stack_rows(rows, total):
    width = rows[0].shape[1]
    sublane = lax.broadcasted_iota(jnp.int32, (total, width), 0)
    result = jnp.zeros((total, width), F32)
    for position, row in enumerate(rows):
        result = jnp.where(sublane == position, row, result)
    return result


def fill_selector(index, wide_ref, fine_ref):
    count, width = wide_ref.shape
    for first in range(0, count, ROWS):
        row = lax.broadcasted_iota(jnp.int32, (ROWS, width), 0) + first
        hit = jnp.where(row == index, 1.0, 0.0)
        wide_ref[pl.ds(first, ROWS), :] = hit.astype(BF16)
        fine_ref[pl.ds(first, ROWS), :] = hit.astype(FINE8)


def cross_kernel(unit, order_ref, jitter_ref, x_ref, upper_ref, lower_ref, high_ref, low_ref, sel_ref, sel8_ref):
    step = pl.program_id(0)
    points = high_ref.shape[1]
    width = upper_ref.shape[1]
    rows = high_ref.shape[0]
    tail = (lax.axis_index("leaf") & 1) == 1

    @pl.when(step == 0)
    def _():
        fill_selector(strip_indices(order_ref, tail, width), sel_ref, sel8_ref)
        upper_ref[rows:, :] = stack_rows(strip_places(jitter_ref, tail, width, unit), 8)

    pieces = points // LANES
    for piece in range(pieces):
        value = x_ref[pl.ds(piece, rows, stride=pieces), :]
        high = value.astype(BF16)
        lanes = pl.ds(piece * LANES, LANES)
        high_ref[:, lanes] = high
        low_ref[:, lanes] = ((value - high.astype(F32)) * LO_UP).astype(WIDE8)
        low_ref[:, pl.ds(points + piece * LANES, LANES)] = (value * FULL_UP).astype(WIDE8)
    picked = dot(high_ref[...], sel_ref[...]) + dot(low_ref[:, :points], sel8_ref[...]) * (1.0 / LO_UP)

    @pl.when(step == 0)
    def _():
        upper_ref[:rows, :] = picked

    @pl.when(step == 1)
    def _():
        lower_ref[...] = picked


def places_kernel(unit, order_ref, jitter_ref, base_ref, spread_ref, base16_ref, base8_ref, far_ref, packed_ref):
    step = pl.program_id(0)
    points = order_ref.shape[1]
    rank = base_ref.shape[0]
    rows = base16_ref.shape[0]

    @pl.when(step == 0)
    def _():
        high, low = split2(base_ref[...])
        packed_ref[0:rank, :] = high
        packed_ref[rank : 2 * rank, :] = low
        index = lax.broadcasted_iota(jnp.int32, (1, points), 1).astype(F32)
        coords = [(index + jitter_ref[0]) * (unit / points), jitter_ref[1] * unit, jitter_ref[2] * unit]
        rest = coords
        pieces = []
        for _ in range(3):
            rounded = [r.astype(BF16).astype(F32) for r in rest]
            pieces.extend(rounded)
            rest = [r - q for r, q in zip(rest, rounded)]
        packed_ref[2 * rank : 2 * rank + 16, :] = stack_rows(pieces, 16).astype(BF16)
        packed_ref[2 * rank + 16 :, :] = jnp.zeros((2 * LANES - 2 * rank - 16, points), BF16)
        far_ref[0:rank, :] = high
        far_ref[rank : 2 * rank, :] = high
        far_ref[2 * rank : 3 * rank, :] = low
        far_ref[3 * rank :, :] = low

    row = lax.broadcasted_iota(jnp.int32, (rows, points), 0) + step * rows
    hit = jnp.where(row == order_ref[...], 1.0, 0.0).astype(BF16)
    moved = lax.dot_general(hit, packed_ref[...], (((1,), (1,)), ((), ())), preferred_element_type=F32)
    both = moved[:, :LANES]
    swap = pltpu.roll(both, LANES // 2, 1)
    left = lax.broadcasted_iota(jnp.int32, (rows, LANES), 1) < LANES // 2
    high = jnp.where(left, both, swap)
    low = jnp.where(left, swap, both)
    base16_ref[:, :LANES] = high.astype(BF16)
    base16_ref[:, LANES:] = low.astype(BF16)
    base8_ref[...] = (high * BASE_UP).astype(FINE8)
    place = moved[:, LANES:]
    place = place + pltpu.roll(place, LANES - 3, 1) + pltpu.roll(place, LANES - 6, 1)
    for component in range(3):
        spread_ref[component] = jnp.broadcast_to(place[:, component : component + 1], (rows, LANES))


def twice(block):
    wide = jnp.concatenate([block, block], axis=1)
    left = lax.broadcasted_iota(jnp.int32, wide.shape, 1) < block.shape[1]
    return jnp.concatenate([jnp.where(left, wide, 0.0), jnp.where(left, 0.0, wide)], axis=0)


def matrices_kernel(leaf_levels, transfer_ref, coupling_ref, lift_ref, couple_ref):
    levels = transfer_ref.shape[0]
    leaf = lax.axis_index("leaf")
    sub = lax.axis_index("sub")
    down = None
    span = 2 * transfer_ref.shape[2]
    for level in range(levels):
        bit = leaf >> level & 1 if level < leaf_levels else sub >> (level - leaf_levels) & 1
        right = bit == 1
        first, second = transfer_ref[level, 0], transfer_ref[level, 1]
        own = jnp.where(right, second, first)
        other = jnp.where(right, first, second)
        couple = jnp.where(right, coupling_ref[level, 1], coupling_ref[level, 0]).T
        if down is not None:
            couple = jnp.dot(couple, down, precision=PRECISE, preferred_element_type=F32)
        high, low = split2(twice(couple))
        couple_ref[pl.ds(level * span, span), :] = high
        couple_ref[pl.ds((levels + level) * span, span), :] = high
        couple_ref[pl.ds((2 * levels + level) * span, span), :] = low
        if level < levels - 1:
            down = own.T if down is None else jnp.dot(own.T, down, precision=PRECISE, preferred_element_type=F32)
            own_high, own_low = split2(twice(own))
            other_high, other_low = split2(twice(other))
            for position, part in enumerate((own_high, other_high, own_high, other_high, own_low, other_low)):
                lift_ref[level, pl.ds(position * span, span), :] = part


def core_kernel(unit, order_ref, jitter_ref, base16_ref, base8_ref, high_ref, low_ref, strip_ref, sel_ref, sel8_ref):
    count, points = high_ref.shape
    width = sel_ref.shape[1]
    tail = (lax.axis_index("leaf") & 1) == 0
    fill_selector(strip_indices(order_ref, tail, width), sel_ref, sel8_ref)
    strip_ref[count:, :width] = stack_rows(strip_places(jitter_ref, tail, width, unit), 8)
    strip_ref[count // 2 :, width:] = jnp.zeros((count // 2 + 8, LANES), F32)
    high = high_ref[...]
    low = low_ref[:, :points]
    moment = dot(high, base16_ref[...])
    moment = moment[:, :LANES] + moment[:, LANES:] + dot(low, base8_ref[...]) * MOMENT_DOWN
    half = GROUP // 2
    left = lax.broadcasted_iota(jnp.int32, (half, LANES), 1) < LANES // 2
    for group in range(count // GROUP):
        first = group * GROUP
        packed = jnp.where(left, moment[first : first + half], moment[first + half : first + GROUP])
        strip_ref[group * half : (group + 1) * half, width:] = packed
    strip_ref[:count, :width] = dot(high, sel_ref[...]) + dot(low, sel8_ref[...]) * (1.0 / LO_UP)


def lift_kernel(own_ref, other_ref, matrix_ref, out_ref):
    own_high, own_low = split2(own_ref[...])
    other_high, other_low = split2(other_ref[...])
    stacked = jnp.concatenate([own_high, other_high, own_low, other_low, own_high, other_high], axis=1)
    out_ref[...] = dot(stacked, matrix_ref[0])


def target_places(jitter_ref, unit, place_ref):
    points = jitter_ref.shape[2]
    index = lax.broadcasted_iota(jnp.int32, (1, points), 1).astype(F32)
    rows = [(index + jitter_ref[0]) * (unit / points), jitter_ref[1] * unit, jitter_ref[2] * unit]
    place_ref[...] = stack_rows(rows, 8)


def fill_weights(unit, place_ref, spread_ref, high_ref, fine_ref, columns, sources):
    root = unit * math.sqrt(DELTA_SQ)
    for block in range(0, sources, ROWS):
        here = pl.ds(block, ROWS)
        for part in range(TILE // LANES):
            lanes = pl.ds(part * LANES, LANES)
            square = root * root
            for component in range(3):
                there = place_ref[component : component + 1, pl.ds(columns + part * LANES, LANES)]
                gap = spread_ref[component, here, :] - there
                square = gap * gap + square
            store_weight(square, high_ref, fine_ref, here, pl.ds(sources + block, ROWS), lanes)


def own_kernel(unit, tiles, chunk, jitter_ref, spread_ref, high_ref, low_ref, *refs):
    out_ref, place_ref, ha, wa, hb, wb = refs[-6:]
    points = high_ref.shape[1]
    target_places(jitter_ref, unit, place_ref)
    buffers = ((ha, wa), (hb, wb))

    def fill(tile):
        high, fine = buffers[tile % 2]
        fill_weights(unit, place_ref, spread_ref, high, fine, (chunk * tiles + tile) * TILE, points)

    fill(0)
    for tile in range(tiles):
        if tile + 1 < tiles:
            fill(tile + 1)
        high, fine = buffers[tile % 2]
        out_ref[chunk, :, tile * TILE : (tile + 1) * TILE] = (
            dot(high_ref[...], high[...]) + dot(low_ref[...], fine[...]) * NEAR_DOWN
        )


def store_weight(square, high_ref, fine_ref, here, there, lanes):
    weight = lax.rsqrt(square)
    high = weight.astype(BF16)
    high_ref[here, lanes] = high
    fine_ref[here, lanes] = (weight * W_UP).astype(FINE8)
    fine_ref[there, lanes] = ((weight - high.astype(F32)) * W_LO_UP).astype(FINE8)


def final_kernel(unit, levels, *refs):
    jitter_ref, core_ref, upper_ref, lower_ref = refs[:4]
    sib_refs = refs[4 : 4 + levels]
    couple_ref, far_ref = refs[4 + levels : 6 + levels]
    near_ref, out_ref, left_ref, low_ref, spread_ref, place_ref, ha, wa, hb, wb, stage_ref, sems = refs[6 + levels :]
    chunks, count, _ = near_ref.shape
    width = upper_ref.shape[1]
    sources = 2 * width

    def fill(tile, high, fine):
        columns = pl.multiple_of(tile * TILE, TILE)
        fill_weights(unit, place_ref, spread_ref, high, fine, columns, sources)
        high[sources:, :] = far_ref[:, pl.ds(columns, TILE)]

    target_places(jitter_ref, unit, place_ref)
    odd = (lax.axis_index("leaf") & 1) == 1
    sign = jnp.where(odd, unit, -unit)

    def place_strip(position, across, shift):
        lanes = pl.ds(position * width, width)
        for component in range(3):
            column = across[:, component : component + 1]
            if component == 0:
                column = column + shift
            spread_ref[component, lanes, :] = jnp.broadcast_to(column, (width, LANES))

    def take_strip(position, rows, value):
        high = value.astype(BF16)
        lanes = pl.ds(position * width, width)
        left_ref[rows, lanes] = high
        low_ref[rows, lanes] = ((value - high.astype(F32)) * LO_UP).astype(WIDE8)
        low_ref[rows, pl.ds(sources + position * width, width)] = (value * FULL_UP).astype(WIDE8)

    place_strip(0, core_ref[count:, :width].T, -sign)
    place_strip(1, upper_ref[count // 2 :, :].T, sign)
    fill(0, ha, wa)
    take_strip(0, pl.ds(0, count), core_ref[:count, :width])
    take_strip(1, pl.ds(0, count // 2), upper_ref[: count // 2, :])
    take_strip(1, pl.ds(count // 2, count // 2), lower_ref[...])
    parts = [split2(sib_refs[0][: count // 2, width:])] + [split2(ref[...]) for ref in sib_refs[1:]]
    stacked = jnp.concatenate([p[0] for p in parts] + [p[1] for p in parts] + [p[0] for p in parts], axis=1)
    expansion = dot(stacked, couple_ref[...])
    high = expansion.astype(BF16).astype(F32)
    low = pltpu.roll(expansion - high, LANES // 2, 1)
    half = GROUP // 2
    is_left = lax.broadcasted_iota(jnp.int32, (half, LANES), 1) < LANES // 2
    for block in range(count // GROUP):
        h = high[block * half : (block + 1) * half]
        l = low[block * half : (block + 1) * half]
        upper = pl.ds(block * GROUP, half)
        lower = pl.ds(block * GROUP + half, half)
        left_ref[upper, sources : sources + LANES] = jnp.where(is_left, h, l).astype(BF16)
        left_ref[lower, sources : sources + LANES] = jnp.where(is_left, l, h).astype(BF16)
        left_ref[upper, sources + LANES :] = jnp.where(is_left, h, 0.0).astype(BF16)
        left_ref[lower, sources + LANES :] = jnp.where(is_left, 0.0, h).astype(BF16)

    parts_per_tile = TILE // LANES

    def copy(pair, tile):
        slot = 2 * (pair % 2) + tile
        lanes = pl.ds((2 * pair + tile) * parts_per_tile, parts_per_tile)
        return pltpu.make_async_copy(
            stage_ref.at[slot].reshape(count, parts_per_tile, LANES), out_ref.at[:, lanes, :], sems.at[slot]
        )

    def product(pair, tile, h, w):
        lanes = slice(tile * TILE, (tile + 1) * TILE)
        value = near_ref[pair, :, lanes] + dot(left_ref[...], h[...]) + dot(low_ref[...], w[...]) * NEAR_DOWN
        for part in range(parts_per_tile):
            stage_ref[2 * (pair % 2) + tile, pl.ds(part, count, stride=parts_per_tile), :] = value[
                :, part * LANES : (part + 1) * LANES
            ]

    def run(pair, carry):
        @pl.when(pair >= 2)
        def _():
            copy(pair - 2, 0).wait()
            copy(pair - 2, 1).wait()

        fill(2 * pair + 1, hb, wb)
        product(pair, 0, ha, wa)
        copy(pair, 0).start()
        fill(jnp.minimum(2 * pair + 2, 2 * chunks - 1), ha, wa)
        product(pair, 1, hb, wb)
        copy(pair, 1).start()
        return carry

    lax.fori_loop(0, chunks, run, 0)
    for pair in range(chunks - 2, chunks):
        copy(pair, 0).wait()
        copy(pair, 1).wait()


def cost(flops, moved):
    return pl.CostEstimate(flops=int(flops), bytes_accessed=int(moved), transcendentals=0)


def whole(array):
    rank = len(array.shape)
    return pl.BlockSpec(array.shape, lambda *_: (0,) * rank)


def shape(dims, dtype=F32):
    return jax.ShapeDtypeStruct(dims, dtype)


def body(charges, ordering, jitter, leaf_bases, transfer, coupling):
    points = charges.shape[4]
    count = charges.shape[0] * charges.shape[1]
    width = points // 4
    rank = leaf_bases.shape[2]
    unit = math.sqrt(points)
    leaf_count = lax.axis_size("leaf")
    sub_count = lax.axis_size("sub")
    leaf_levels = leaf_count.bit_length() - 1
    sub_levels = sub_count.bit_length() - 1
    levels = leaf_levels + sub_levels
    half = count // 2
    pieces = points // LANES
    x = charges.reshape(count * pieces, LANES)
    order = ordering.reshape(1, points)
    offsets = jitter.reshape(3, 1, points)
    base = leaf_bases.reshape(rank, points)
    params = lambda mib: pltpu.CompilerParams(vmem_limit_bytes=mib << 20)
    vmem = pl.BlockSpec(memory_space=pltpu.VMEM)

    upper, lower, high, low = pl.pallas_call(
        functools.partial(cross_kernel, unit),
        grid=(2,),
        in_specs=[whole(order), whole(offsets), pl.BlockSpec((half * pieces, LANES), lambda i: (i, 0))],
        out_specs=[
            pl.BlockSpec((half + 8, width), lambda i: (0, 0)),
            pl.BlockSpec((half, width), lambda i: (0, 0)),
            pl.BlockSpec((half, points), lambda i: (i, 0)),
            pl.BlockSpec((half, 2 * points), lambda i: (i, 0)),
        ],
        out_shape=[
            shape((half + 8, width)),
            shape((half, width)),
            shape((count, points), BF16),
            shape((count, 2 * points), WIDE8),
        ],
        scratch_shapes=[pltpu.VMEM((points, width), BF16), pltpu.VMEM((points, width), FINE8)],
        compiler_params=params(30),
        cost_estimate=cost(3 * count * points * width, 16 * count * points),
        name="cross",
    )(order, offsets, pltpu.with_memory_space_constraint(x, pltpu.HBM))
    last = leaf_count - 1
    middle = leaf_count // 2
    up_pairs = [(i, i + 1) for i in range(1, last, 2)]
    direct = up_pairs + [(b, a) for a, b in up_pairs]
    ends = (0, middle - 1, middle, last)
    to_relay = [(middle - 1, last), (middle, 0)] + [(i, i) for i in range(leaf_count) if i not in ends]
    relayed = [p for p in direct if p[0] not in ends] + [(last, middle), (0, middle - 1)]
    if leaf_count < 4:
        to_relay, relayed = [], []
    upper_in = lax.ppermute(upper, "leaf", direct)
    relay = lax.ppermute(lower, "leaf", to_relay)

    spread, base16, base8, far = pl.pallas_call(
        functools.partial(places_kernel, unit),
        grid=(points // GROUP,),
        in_specs=[whole(order), whole(offsets), whole(base)],
        out_specs=[
            pl.BlockSpec((3, GROUP, LANES), lambda i: (0, i, 0)),
            pl.BlockSpec((GROUP, 2 * LANES), lambda i: (i, 0)),
            pl.BlockSpec((GROUP, LANES), lambda i: (i, 0)),
            pl.BlockSpec((4 * rank, points), lambda i: (0, 0)),
        ],
        out_shape=[
            shape((3, points, LANES)),
            shape((points, 2 * LANES), BF16),
            shape((points, LANES), FINE8),
            shape((4 * rank, points), BF16),
        ],
        scratch_shapes=[pltpu.VMEM((2 * LANES, points), BF16)],
        compiler_params=params(16),
        cost_estimate=cost(2 * points * points * 256, 5 * points * 1024),
        name="places",
    )(order, offsets, base)

    core = pl.pallas_call(
        functools.partial(core_kernel, unit),
        in_specs=[vmem] * 6,
        out_specs=vmem,
        out_shape=shape((count + 8, width + LANES)),
        scratch_shapes=[pltpu.VMEM((points, width), BF16), pltpu.VMEM((points, width), FINE8)],
        compiler_params=params(16),
        cost_estimate=cost(3 * count * points * (width + 256), 6 * count * points),
        name="core",
    )(order, offsets, base16, base8, high, low)
    core_in = lax.ppermute(core, "leaf", [(i, i ^ 1) for i in range(leaf_count)])

    lift, couple = pl.pallas_call(
        functools.partial(matrices_kernel, leaf_levels),
        in_specs=[vmem] * 2,
        out_specs=[vmem] * 2,
        out_shape=[shape((levels - 1, 12 * rank, 2 * rank), BF16), shape((6 * levels * rank, 2 * rank), BF16)],
        compiler_params=params(8),
        cost_estimate=cost(1e6, 1e6),
        name="matrices",
    )(transfer, coupling)

    tiles = 2
    chunks = points // (tiles * TILE)
    near = None

    def own(chunk, near):
        operands = (offsets, spread, high, low) + (() if near is None else (near,))
        return pl.pallas_call(
            functools.partial(own_kernel, unit, tiles, chunk),
            in_specs=[vmem] * 4 + ([] if near is None else [pl.BlockSpec(memory_space=pl.ANY)]),
            out_specs=vmem,
            out_shape=shape((chunks, count, tiles * TILE)),
            scratch_shapes=[pltpu.VMEM((8, points), F32)]
            + [pltpu.VMEM((points, TILE), BF16), pltpu.VMEM((2 * points, TILE), FINE8)] * 2,
            input_output_aliases={} if near is None else {4: 0},
            compiler_params=params(12),
            cost_estimate=cost(4 * count * points * tiles * TILE, 10 * count * points),
        )(*operands)

    def lifted(level, own_moment, other, from_strip):
        spec = pl.BlockSpec((half, LANES), (lambda i: (0, width // LANES)) if from_strip else (lambda i: (0, 0)))
        return pl.pallas_call(
            lift_kernel,
            grid=(1,),
            in_specs=[spec, spec, pl.BlockSpec((1, 12 * rank, 2 * rank), lambda i: (level, 0, 0))],
            out_specs=pl.BlockSpec((half, LANES), lambda i: (0, 0)),
            out_shape=shape((half, LANES)),
            compiler_params=params(8),
            cost_estimate=cost(2 * half * 768 * 128, 3 * half * 512),
        )(own_moment, other, lift)

    near = own(0, None)
    siblings = [core_in]
    current = core
    for level in range(1, levels):
        current = lifted(level - 1, current, siblings[-1], level == 1)
        axis, bit = ("leaf", level) if level < leaf_levels else ("sub", level - leaf_levels)
        pairs = [(i, i ^ 1 << bit) for i in range(lax.axis_size(axis))]
        siblings.append(lax.ppermute(current, axis, pairs))
        if level == 1:
            lower_in = lax.ppermute(relay, "leaf", relayed)
        if level < chunks:
            near = own(level, near)
    for chunk in range(levels, chunks):
        near = own(chunk, near)

    sources = 2 * width
    out = pl.pallas_call(
        functools.partial(final_kernel, unit, levels),
        in_specs=[vmem] * (7 + levels),
        out_specs=pl.BlockSpec(memory_space=pl.ANY),
        out_shape=shape((count, pieces, LANES)),
        scratch_shapes=[
            pltpu.VMEM((count, sources + 4 * rank), BF16),
            pltpu.VMEM((count, 2 * sources), WIDE8),
            pltpu.VMEM((3, sources, LANES), F32),
            pltpu.VMEM((8, points), F32),
        ]
        + [pltpu.VMEM((sources + 4 * rank, TILE), BF16), pltpu.VMEM((2 * sources, TILE), FINE8)] * 2
        + [pltpu.VMEM((4, count * TILE // LANES, LANES), F32), pltpu.SemaphoreType.DMA((4,))],
        compiler_params=params(24),
        cost_estimate=cost(4 * count * points * sources, 8 * count * points),
        name="final",
    )(offsets, core_in, upper_in, lower_in, *siblings, couple, far, near)
    return out.reshape(charges.shape)


def solution(mesh):
    in_specs = (
        P(None, None, "sub", "leaf", None),
        P("sub", "leaf", None),
        P(None, "sub", "leaf", None),
        P("sub", "leaf", None, None),
        P(),
        P(),
    )
    out_specs = P(None, None, "sub", "leaf", None)

    return jax.shard_map(body, mesh=mesh, in_specs=in_specs, out_specs=out_specs, check_vma=False)
```

```python
import functools
import math

import jax
import jax.numpy as jnp
from jax import lax
from jax.experimental import pallas as pl
from jax.experimental.pallas import tpu as pltpu
from jax.sharding import PartitionSpec as P


DELTA_SQ = 0.0025
PRECISE = lax.Precision.HIGHEST
LANES = 128
ROWS = 256
GROUP = 512
TILE = 256
BF16 = jnp.bfloat16
F32 = jnp.float32
WIDE8 = jnp.float8_e5m2
FINE8 = jnp.float8_e4m3fn
LO_UP = 2.0**20
FULL_UP = 2.0**13
W_UP = 2.0**9
W_LO_UP = 2.0**16
NEAR_DOWN = 2.0**-29
BASE_UP = 2.0**10
MOMENT_DOWN = 2.0**-30


def dot(a, b):
    return jnp.dot(a, b, preferred_element_type=F32)


def split2(value):
    high = value.astype(BF16)
    return high, (value - high.astype(F32)).astype(BF16)


def remainders(value, high):
    rest = (value - high.astype(F32)).astype(BF16)
    return (rest * BF16(LO_UP)).astype(WIDE8), (high * BF16(FULL_UP)).astype(WIDE8)


def strip_indices(order_ref, tail, width):
    count = order_ref.shape[1]
    return jnp.where(tail, order_ref[:, count - width :], order_ref[:, :width])


def strip_places(jitter_ref, tail, width, unit):
    count = jitter_ref.shape[2]

    def part(component):
        row = jitter_ref[component]
        return jnp.where(tail, row[:, count - width :], row[:, :width])

    start = jnp.where(tail, count - width, 0)
    index = (lax.broadcasted_iota(jnp.int32, (1, width), 1) + start).astype(F32)
    along = (index + part(0)) * (unit / count)
    return along, part(1) * unit, part(2) * unit


def stack_rows(rows, total):
    width = rows[0].shape[1]
    sublane = lax.broadcasted_iota(jnp.int32, (total, width), 0)
    result = jnp.zeros((total, width), F32)
    for position, row in enumerate(rows):
        result = jnp.where(sublane == position, row, result)
    return result


def fill_selector(index, wide_ref, fine_ref):
    count, width = wide_ref.shape
    for first in range(0, count, ROWS):
        row = lax.broadcasted_iota(jnp.int32, (ROWS, width), 0) + first
        hit = jnp.where(row == index, 1.0, 0.0)
        wide_ref[pl.ds(first, ROWS), :] = hit.astype(BF16)
        fine_ref[pl.ds(first, ROWS), :] = hit.astype(FINE8)


def cross_kernel(unit, order_ref, jitter_ref, x_ref, upper_ref, lower_ref, high_ref, low_ref, sel_ref, sel8_ref, x_buf, sems):
    count, points = high_ref.shape
    width = upper_ref.shape[1]
    pieces = points // LANES
    parts = x_buf.shape[0]
    rows = count // parts
    tail = (lax.axis_index("leaf") & 1) == 1

    def copies(part):
        here = pl.ds(part * rows, rows)
        return [
            pltpu.make_async_copy(x_ref.at[here, piece, :], x_buf.at[part, piece], sems.at[part, piece])
            for piece in range(pieces)
        ]

    def split(part):
        here = pl.ds(pl.multiple_of(part * rows, rows), rows)
        for piece in range(pieces):
            value = x_buf[part, piece]
            high = value.astype(BF16)
            lanes = pl.ds(piece * LANES, LANES)
            high_ref[here, lanes] = high
            low_ref[here, lanes], low_ref[here, pl.ds(points + piece * LANES, LANES)] = remainders(value, high)

    def pick(first, size):
        here = pl.ds(first, size)
        return dot(high_ref[here, :], sel_ref[...]) + dot(low_ref[here, :points], sel8_ref[...]) * (1.0 / LO_UP)

    for part in range(parts):
        for copy in copies(part):
            copy.start()
    half = count // 2
    fill_selector(strip_indices(order_ref, tail, width), sel_ref, sel8_ref)
    upper_ref[half:, :] = stack_rows(strip_places(jitter_ref, tail, width, unit), 8)

    def early(part, carry):
        for copy in copies(part):
            copy.wait()
        split(part)
        return carry

    lax.fori_loop(0, parts // 2, early, 0)
    for part in range(parts // 2, parts):
        for copy in copies(part):
            copy.wait()
    for part in range(parts // 2, parts):
        split(part)
    upper_ref[:half, :] = pick(0, half)
    lower_ref[...] = pick(half, half)


def places_kernel(unit, order_ref, jitter_ref, base_ref, spread_ref, base16_ref, base8_ref, far_ref, packed_ref):
    step = pl.program_id(0)
    points = order_ref.shape[1]
    rank = base_ref.shape[0]
    rows = base16_ref.shape[0]

    @pl.when(step == 0)
    def _():
        high, low = split2(base_ref[...])
        packed_ref[0:rank, :] = high
        packed_ref[rank : 2 * rank, :] = low
        index = lax.broadcasted_iota(jnp.int32, (1, points), 1).astype(F32)
        coords = [(index + jitter_ref[0]) * (unit / points), jitter_ref[1] * unit, jitter_ref[2] * unit]
        rest = coords
        pieces = []
        for _ in range(3):
            rounded = [r.astype(BF16).astype(F32) for r in rest]
            pieces.extend(rounded)
            rest = [r - q for r, q in zip(rest, rounded)]
        packed_ref[2 * rank : 2 * rank + 16, :] = stack_rows(pieces, 16).astype(BF16)
        packed_ref[2 * rank + 16 :, :] = jnp.zeros((2 * LANES - 2 * rank - 16, points), BF16)
        far_ref[0:rank, :] = high
        far_ref[rank : 2 * rank, :] = high
        far_ref[2 * rank : 3 * rank, :] = low
        far_ref[3 * rank :, :] = low

    row = lax.broadcasted_iota(jnp.int32, (rows, points), 0) + step * rows
    hit = jnp.where(row == order_ref[...], 1.0, 0.0).astype(BF16)
    moved = lax.dot_general(hit, packed_ref[...], (((1,), (1,)), ((), ())), preferred_element_type=F32)
    both = moved[:, :LANES]
    swap = pltpu.roll(both, LANES // 2, 1)
    left = lax.broadcasted_iota(jnp.int32, (rows, LANES), 1) < LANES // 2
    high = jnp.where(left, both, swap)
    low = jnp.where(left, swap, both)
    base16_ref[:, :LANES] = high.astype(BF16)
    base16_ref[:, LANES:] = low.astype(BF16)
    base8_ref[...] = (high * BASE_UP).astype(FINE8)
    place = moved[:, LANES:]
    place = place + pltpu.roll(place, LANES - 3, 1) + pltpu.roll(place, LANES - 6, 1)
    for component in range(3):
        spread_ref[component] = jnp.broadcast_to(place[:, component : component + 1], (rows, LANES))


def twice(block):
    wide = jnp.concatenate([block, block], axis=1)
    left = lax.broadcasted_iota(jnp.int32, wide.shape, 1) < block.shape[1]
    return jnp.concatenate([jnp.where(left, wide, 0.0), jnp.where(left, 0.0, wide)], axis=0)


def matrices_kernel(leaf_levels, transfer_ref, coupling_ref, lift_ref, couple_ref, last_ref):
    levels = transfer_ref.shape[0]
    leaf = lax.axis_index("leaf")
    sub = lax.axis_index("sub")
    down = None
    span = 2 * transfer_ref.shape[2]
    upper = levels - 1
    for level in range(levels):
        bit = leaf >> level & 1 if level < leaf_levels else sub >> (level - leaf_levels) & 1
        right = bit == 1
        first, second = transfer_ref[level, 0], transfer_ref[level, 1]
        own = jnp.where(right, second, first)
        other = jnp.where(right, first, second)
        couple = jnp.where(right, coupling_ref[level, 1], coupling_ref[level, 0]).T
        if down is not None:
            couple = jnp.dot(couple, down, precision=PRECISE, preferred_element_type=F32)
        high, low = split2(twice(couple))
        if level == 0:
            step_high, step_low = split2(twice(own.T))
            for position, part in enumerate((high, step_high, high, step_high, low, step_low)):
                last_ref[pl.ds(position * span, span), :] = part
        else:
            couple_ref[pl.ds((level - 1) * span, span), :] = high
            couple_ref[pl.ds((upper + level - 1) * span, span), :] = high
            couple_ref[pl.ds((2 * upper + level - 1) * span, span), :] = low
        if level < levels - 1:
            if level > 0:
                down = own.T if down is None else jnp.dot(own.T, down, precision=PRECISE, preferred_element_type=F32)
            own_high, own_low = split2(twice(own))
            other_high, other_low = split2(twice(other))
            for position, part in enumerate((own_high, other_high, own_high, other_high, own_low, other_low)):
                lift_ref[level, pl.ds(position * span, span), :] = part


def core_kernel(unit, order_ref, jitter_ref, base16_ref, base8_ref, high_ref, low_ref, strip_ref, sel_ref, sel8_ref):
    count, points = high_ref.shape
    width = sel_ref.shape[1]
    tail = (lax.axis_index("leaf") & 1) == 0
    fill_selector(strip_indices(order_ref, tail, width), sel_ref, sel8_ref)
    strip_ref[count:, :width] = stack_rows(strip_places(jitter_ref, tail, width, unit), 8)
    strip_ref[count // 2 :, width:] = jnp.zeros((count // 2 + 8, LANES), F32)
    high = high_ref[...]
    low = low_ref[:, :points]
    moment = dot(high, base16_ref[...])
    moment = moment[:, :LANES] + moment[:, LANES:] + dot(low, base8_ref[...]) * MOMENT_DOWN
    half = GROUP // 2
    left = lax.broadcasted_iota(jnp.int32, (half, LANES), 1) < LANES // 2
    for group in range(count // GROUP):
        first = group * GROUP
        packed = jnp.where(left, moment[first : first + half], moment[first + half : first + GROUP])
        strip_ref[group * half : (group + 1) * half, width:] = packed
    strip_ref[:count, :width] = dot(high, sel_ref[...]) + dot(low, sel8_ref[...]) * (1.0 / LO_UP)


def split_product(values, matrix):
    parts = [split2(value) for value in values]
    stacked = [p[0] for p in parts] + [p[1] for p in parts] + [p[0] for p in parts]
    return dot(jnp.concatenate(stacked, axis=1), matrix)


def lift_kernel(level, own_ref, other_ref, matrix_ref, out_ref):
    out_ref[...] = split_product([own_ref[...], other_ref[...]], matrix_ref[level])


def first_lift_kernel(own_ref, other_ref, matrix_ref, out_ref):
    rows = out_ref.shape[0]
    width = own_ref.shape[1] - LANES
    here = pl.ds(pl.multiple_of((lax.axis_index("leaf") & 1) * rows, rows), rows)
    out_ref[...] = split_product([own_ref[here, width:], other_ref[here, width:]], matrix_ref[0])


def collect_kernel(*refs):
    sib_refs, couple_ref, out_ref = refs[:-2], refs[-2], refs[-1]
    out_ref[...] = split_product([ref[...] for ref in sib_refs], couple_ref[...])


def target_places(jitter_ref, unit, place_ref):
    points = jitter_ref.shape[2]
    index = lax.broadcasted_iota(jnp.int32, (1, points), 1).astype(F32)
    rows = [(index + jitter_ref[0]) * (unit / points), jitter_ref[1] * unit, jitter_ref[2] * unit]
    place_ref[...] = stack_rows(rows, 8)


def fill_weights(unit, place_ref, spread_ref, high_ref, fine_ref, columns, sources, looped=False):
    root = unit * math.sqrt(DELTA_SQ)

    def one(block):
        here = pl.ds(block, ROWS)
        for part in range(TILE // LANES):
            lanes = pl.ds(part * LANES, LANES)
            square = root * root
            for component in range(3):
                there = place_ref[component : component + 1, pl.ds(columns + part * LANES, LANES)]
                gap = spread_ref[component, here, :] - there
                square = gap * gap + square
            store_weight(square, high_ref, fine_ref, here, pl.ds(sources + block, ROWS), lanes)

    if looped:

        def run(index, carry):
            one(pl.multiple_of(index * ROWS, ROWS))
            return carry

        lax.fori_loop(0, sources // ROWS, run, 0)
    else:
        for block in range(0, sources, ROWS):
            one(block)


def own_kernel(unit, chunk, jitter_ref, spread_ref, high_ref, low_ref, *refs):
    out_ref, ha, wa, place_ref, hb, wb = refs[-6:]
    chunks = out_ref.shape[0]
    points = high_ref.shape[1]
    target_places(jitter_ref, unit, place_ref)

    def fill(tile, high, fine, looped=False):
        fill_weights(unit, place_ref, spread_ref, high, fine, tile * TILE, points, looped)

    def product(tile, high, fine):
        value = dot(high_ref[...], high[...]) + dot(low_ref[...], fine[...]) * NEAR_DOWN
        out_ref[chunk, :, tile * TILE : (tile + 1) * TILE] = value

    if chunk == 0:
        fill(0, ha, wa, True)
    fill(2 * chunk + 1, hb, wb)
    product(0, ha, wa)
    if chunk + 1 < chunks:
        fill(2 * chunk + 2, ha, wa)
    product(1, hb, wb)


def store_weight(square, high_ref, fine_ref, here, there, lanes):
    weight = lax.rsqrt(square)
    high = weight.astype(BF16)
    high_ref[here, lanes] = high
    fine_ref[here, lanes] = (high * BF16(W_UP)).astype(FINE8)
    rest = (weight - high.astype(F32)).astype(BF16)
    fine_ref[there, lanes] = (rest * BF16(W_LO_UP)).astype(FINE8)


def place_strip(spread_ref, across, shift):
    for component in range(3):
        column = across[:, component : component + 1]
        if component == 0:
            column = column + shift
        spread_ref[component] = jnp.broadcast_to(column, spread_ref.shape[1:])


def take_strip(left_ref, low_ref, rows, value):
    width = value.shape[1]
    high = value.astype(BF16)
    left_ref[rows, :width] = high
    low_ref[rows, :width], low_ref[rows, width:] = remainders(value, high)


def core_shift(unit):
    odd = (lax.axis_index("leaf") & 1) == 1
    return jnp.where(odd, -unit, unit)


def middle_kernel(unit, jitter_ref, core_ref, near_ref, out_ref, left_ref, low_ref, spread_ref, place_ref, ha, wa, hb, wb):
    chunks, count, _ = near_ref.shape
    width = left_ref.shape[1]
    target_places(jitter_ref, unit, place_ref)
    place_strip(spread_ref, core_ref[count:, :width].T, core_shift(unit))

    def fill(tile, high, fine):
        fill_weights(unit, place_ref, spread_ref, high, fine, pl.multiple_of(tile * TILE, TILE), width)

    fill_weights(unit, place_ref, spread_ref, ha, wa, 0, width, True)
    take_strip(left_ref, low_ref, pl.ds(0, count), core_ref[:count, :width])

    def product(pair, tile, h, w):
        lanes = slice(tile * TILE, (tile + 1) * TILE)
        out_ref[pair, :, lanes] = (
            near_ref[pair, :, lanes] + dot(left_ref[...], h[...]) + dot(low_ref[...], w[...]) * NEAR_DOWN
        )

    def run(pair, carry):
        fill(2 * pair + 1, hb, wb)
        product(pair, 0, ha, wa)
        fill(jnp.minimum(2 * pair + 2, 2 * chunks - 1), ha, wa)
        product(pair, 1, hb, wb)
        return carry

    lax.fori_loop(0, chunks, run, 0)


def final_kernel(unit, jitter_ref, core_ref, upper_ref, lower_ref, mine_ref, other_ref, last_ref, far_ref, near_ref, *refs):
    out_ref, left_ref, low_ref, spread_ref, place_ref, ha, wa, hb, wb, stage_ref, sems = refs
    chunks, count, _ = near_ref.shape
    width = upper_ref.shape[1]

    def fill(tile, high, fine):
        columns = pl.multiple_of(tile * TILE, TILE)
        fill_weights(unit, place_ref, spread_ref, high, fine, columns, width)
        high[width:, :] = far_ref[:, pl.ds(columns, TILE)]

    target_places(jitter_ref, unit, place_ref)
    place_strip(spread_ref, upper_ref[count // 2 :, :].T, -core_shift(unit))
    fill(0, ha, wa)
    take_strip(left_ref.at[:, pl.ds(0, width)], low_ref, pl.ds(0, count // 2), upper_ref[: count // 2, :])
    take_strip(left_ref.at[:, pl.ds(0, width)], low_ref, pl.ds(count // 2, count // 2), lower_ref[...])
    even = (lax.axis_index("leaf") & 1) == 0
    mine, other = mine_ref[...], other_ref[...]
    above = jnp.concatenate([jnp.where(even, mine, other), jnp.where(even, other, mine)], axis=0)
    expansion = split_product([core_ref[: count // 2, width:], above], last_ref[...])
    high = expansion.astype(BF16).astype(F32)
    low = pltpu.roll(expansion - high, LANES // 2, 1)
    half = GROUP // 2
    is_left = lax.broadcasted_iota(jnp.int32, (half, LANES), 1) < LANES // 2
    for block in range(count // GROUP):
        h = high[block * half : (block + 1) * half]
        l = low[block * half : (block + 1) * half]
        first = pl.ds(block * GROUP, half)
        second = pl.ds(block * GROUP + half, half)
        left_ref[first, width : width + LANES] = jnp.where(is_left, h, l).astype(BF16)
        left_ref[second, width : width + LANES] = jnp.where(is_left, l, h).astype(BF16)
        left_ref[first, width + LANES :] = jnp.where(is_left, h, 0.0).astype(BF16)
        left_ref[second, width + LANES :] = jnp.where(is_left, 0.0, h).astype(BF16)

    parts_per_tile = TILE // LANES

    def copy(pair, tile):
        slot = 2 * (pair % 2) + tile
        lanes = pl.ds((2 * pair + tile) * parts_per_tile, parts_per_tile)
        return pltpu.make_async_copy(
            stage_ref.at[slot].reshape(count, parts_per_tile, LANES), out_ref.at[:, lanes, :], sems.at[slot]
        )

    def product(pair, tile, h, w):
        lanes = slice(tile * TILE, (tile + 1) * TILE)
        value = near_ref[pair, :, lanes] + dot(left_ref[...], h[...]) + dot(low_ref[...], w[...]) * NEAR_DOWN
        for part in range(parts_per_tile):
            stage_ref[2 * (pair % 2) + tile, pl.ds(part, count, stride=parts_per_tile), :] = value[
                :, part * LANES : (part + 1) * LANES
            ]

    def run(pair, carry):
        @pl.when(pair >= 2)
        def _():
            copy(pair - 2, 0).wait()
            copy(pair - 2, 1).wait()

        fill(2 * pair + 1, hb, wb)
        product(pair, 0, ha, wa)
        copy(pair, 0).start()
        fill(jnp.minimum(2 * pair + 2, 2 * chunks - 1), ha, wa)
        product(pair, 1, hb, wb)
        copy(pair, 1).start()
        return carry

    lax.fori_loop(0, chunks, run, 0)
    for pair in range(chunks - 2, chunks):
        copy(pair, 0).wait()
        copy(pair, 1).wait()


def cost(flops, moved):
    return pl.CostEstimate(flops=int(flops), bytes_accessed=int(moved), transcendentals=0)


def whole(array):
    rank = len(array.shape)
    return pl.BlockSpec(array.shape, lambda *_: (0,) * rank)


def shape(dims, dtype=F32):
    return jax.ShapeDtypeStruct(dims, dtype)


def body(charges, ordering, jitter, leaf_bases, transfer, coupling):
    points = charges.shape[4]
    count = charges.shape[0] * charges.shape[1]
    width = points // 4
    rank = leaf_bases.shape[2]
    unit = math.sqrt(points)
    leaf_count = lax.axis_size("leaf")
    sub_count = lax.axis_size("sub")
    leaf_levels = leaf_count.bit_length() - 1
    sub_levels = sub_count.bit_length() - 1
    levels = leaf_levels + sub_levels
    half = count // 2
    pieces = points // LANES
    x = charges.reshape(count, pieces, LANES)
    order = ordering.reshape(1, points)
    offsets = jitter.reshape(3, 1, points)
    base = leaf_bases.reshape(rank, points)
    params = lambda mib: pltpu.CompilerParams(vmem_limit_bytes=mib << 20)
    vmem = pl.BlockSpec(memory_space=pltpu.VMEM)

    in_hbm = lambda array: pltpu.with_memory_space_constraint(array, pltpu.HBM)
    parts = 4
    upper, lower, high, low = pl.pallas_call(
        functools.partial(cross_kernel, unit),
        in_specs=[vmem, vmem, pl.BlockSpec(memory_space=pltpu.HBM)],
        out_specs=[vmem] * 4,
        out_shape=[
            shape((half + 8, width)),
            shape((half, width)),
            shape((count, points), BF16),
            shape((count, 2 * points), WIDE8),
        ],
        scratch_shapes=[
            pltpu.VMEM((points, width), BF16),
            pltpu.VMEM((points, width), FINE8),
            pltpu.VMEM((parts, pieces, count // parts, LANES), F32),
            pltpu.SemaphoreType.DMA((parts, pieces)),
        ],
        compiler_params=params(20),
        cost_estimate=cost(3 * count * points * width, 16 * count * points),
        name="cross",
    )(order, offsets, in_hbm(x))
    last = leaf_count - 1
    middle = leaf_count // 2
    up_pairs = [(i, i + 1) for i in range(1, last, 2)]
    direct = up_pairs + [(b, a) for a, b in up_pairs]
    ends = (0, middle - 1, middle, last)
    to_relay = [(middle - 1, last), (middle, 0)] + [(i, i) for i in range(leaf_count) if i not in ends]
    relayed = [p for p in direct if p[0] not in ends] + [(last, middle), (0, middle - 1)]
    if leaf_count < 4:
        to_relay, relayed = [], []
    upper_in = lax.ppermute(upper, "leaf", direct)
    relay = lax.ppermute(lower, "leaf", to_relay)

    spread, base16, base8, far = pl.pallas_call(
        functools.partial(places_kernel, unit),
        grid=(points // GROUP,),
        in_specs=[whole(order), whole(offsets), whole(base)],
        out_specs=[
            pl.BlockSpec((3, GROUP, LANES), lambda i: (0, i, 0)),
            pl.BlockSpec((GROUP, 2 * LANES), lambda i: (i, 0)),
            pl.BlockSpec((GROUP, LANES), lambda i: (i, 0)),
            pl.BlockSpec((4 * rank, points), lambda i: (0, 0)),
        ],
        out_shape=[
            shape((3, points, LANES)),
            shape((points, 2 * LANES), BF16),
            shape((points, LANES), FINE8),
            shape((4 * rank, points), BF16),
        ],
        scratch_shapes=[pltpu.VMEM((2 * LANES, points), BF16)],
        compiler_params=params(16),
        cost_estimate=cost(2 * points * points * 256, 5 * points * 1024),
        name="places",
    )(order, offsets, base)

    core = pl.pallas_call(
        functools.partial(core_kernel, unit),
        in_specs=[vmem] * 6,
        out_specs=vmem,
        out_shape=shape((count + 8, width + LANES)),
        scratch_shapes=[pltpu.VMEM((points, width), BF16), pltpu.VMEM((points, width), FINE8)],
        compiler_params=params(16),
        cost_estimate=cost(3 * count * points * (width + 256), 6 * count * points),
        name="core",
    )(order, offsets, base16, base8, high, low)
    core_in = lax.ppermute(core, "leaf", [(i, i ^ 1) for i in range(leaf_count)])

    lift, couple, last_matrix = pl.pallas_call(
        functools.partial(matrices_kernel, leaf_levels),
        in_specs=[vmem] * 2,
        out_specs=[vmem] * 3,
        out_shape=[
            shape((levels - 1, 12 * rank, 2 * rank), BF16),
            shape((6 * (levels - 1) * rank, 2 * rank), BF16),
            shape((12 * rank, 2 * rank), BF16),
        ],
        compiler_params=params(8),
        cost_estimate=cost(1e6, 1e6),
        name="matrices",
    )(transfer, coupling)

    chunks = points // (2 * TILE)

    def own(chunk, *carried):
        return pl.pallas_call(
            functools.partial(own_kernel, unit, chunk),
            in_specs=[vmem] * 4 + [pl.BlockSpec(memory_space=pl.ANY)] * len(carried),
            out_specs=[vmem] * 3,
            out_shape=[shape((chunks, count, 2 * TILE)), shape((points, TILE), BF16), shape((2 * points, TILE), FINE8)],
            scratch_shapes=[
                pltpu.VMEM((8, points), F32),
                pltpu.VMEM((points, TILE), BF16),
                pltpu.VMEM((2 * points, TILE), FINE8),
            ],
            input_output_aliases={4 + i: i for i in range(len(carried))},
            compiler_params=params(8),
            cost_estimate=cost(8 * count * points * TILE, 10 * count * points),
        )(offsets, spread, high, low, *carried)

    quarter = half // 2

    def small(kernel, operands):
        return pl.pallas_call(
            kernel,
            in_specs=[vmem] * len(operands),
            out_specs=vmem,
            out_shape=shape((quarter, LANES)),
            compiler_params=params(4),
            cost_estimate=cost(2 * quarter * 768 * 128, 3 * quarter * 512),
        )(*operands)

    carried = own(0)
    siblings = []
    current = small(first_lift_kernel, (core, core_in, lift))
    for level in range(1, levels):
        if level > 1:
            kernel = functools.partial(lift_kernel, level - 1)
            current = small(kernel, (current, siblings[-1], lift))
        axis, bit = ("leaf", level) if level < leaf_levels else ("sub", level - leaf_levels)
        pairs = [(i, i ^ 1 << bit) for i in range(lax.axis_size(axis))]
        siblings.append(lax.ppermute(current, axis, pairs))
        if level == 1:
            lower_in = lax.ppermute(relay, "leaf", relayed)
        if level < chunks:
            carried = own(level, *carried)
    for chunk in range(levels, chunks):
        carried = own(chunk, *carried)
    mine = small(collect_kernel, (*siblings, couple))
    other = lax.ppermute(mine, "leaf", [(i, i ^ 1) for i in range(leaf_count)])

    def strip_scratch(extra):
        tall = width + extra
        return [
            pltpu.VMEM((count, tall), BF16),
            pltpu.VMEM((count, 2 * width), WIDE8),
            pltpu.VMEM((3, width, LANES), F32),
            pltpu.VMEM((8, points), F32),
        ] + [pltpu.VMEM((tall, TILE), BF16), pltpu.VMEM((2 * width, TILE), FINE8)] * 2

    near = pl.pallas_call(
        functools.partial(middle_kernel, unit),
        in_specs=[vmem] * 3,
        out_specs=vmem,
        out_shape=shape((chunks, count, 2 * TILE)),
        scratch_shapes=strip_scratch(0),
        input_output_aliases={2: 0},
        compiler_params=params(12),
        cost_estimate=cost(4 * count * points * width, 8 * count * points),
        name="middle",
    )(offsets, core_in, carried[0])

    out = pl.pallas_call(
        functools.partial(final_kernel, unit),
        in_specs=[vmem] * 9,
        out_specs=pl.BlockSpec(memory_space=pl.ANY),
        out_shape=shape((count, pieces, LANES)),
        scratch_shapes=strip_scratch(4 * rank)
        + [pltpu.VMEM((4, count * TILE // LANES, LANES), F32), pltpu.SemaphoreType.DMA((4,))],
        compiler_params=params(20),
        cost_estimate=cost(4 * count * points * width, 8 * count * points),
        name="final",
    )(offsets, core_in, upper_in, lower_in, mine, other, last_matrix, far, near)
    return out.reshape(charges.shape)


def solution(mesh):
    in_specs = (
        P(None, None, "sub", "leaf", None),
        P("sub", "leaf", None),
        P(None, "sub", "leaf", None),
        P("sub", "leaf", None, None),
        P(),
        P(),
    )
    out_specs = P(None, None, "sub", "leaf", None)

    return jax.shard_map(body, mesh=mesh, in_specs=in_specs, out_specs=out_specs, check_vma=False)
```

```python
import functools
import math

import jax
import jax.numpy as jnp
from jax import lax
from jax.experimental import pallas as pl
from jax.experimental.pallas import tpu as pltpu
from jax.sharding import PartitionSpec as P


DELTA_SQ = 0.0025
PRECISE = lax.Precision.HIGHEST
LANES = 128
ROWS = 256
GROUP = 512
TILE = 256
BF16 = jnp.bfloat16
F32 = jnp.float32
WIDE8 = jnp.float8_e5m2
FINE8 = jnp.float8_e4m3fn
LO_UP = 2.0**20
FULL_UP = 2.0**13
W_UP = 2.0**9
W_LO_UP = 2.0**16
NEAR_DOWN = 2.0**-29
BASE_UP = 2.0**10
MOMENT_DOWN = 2.0**-30


def dot(a, b):
    return jnp.dot(a, b, preferred_element_type=F32)


def split2(value):
    high = value.astype(BF16)
    return high, (value - high.astype(F32)).astype(BF16)


def remainders(value, high):
    rest = (value - high.astype(F32)).astype(BF16)
    return (rest * BF16(LO_UP)).astype(WIDE8), (high * BF16(FULL_UP)).astype(WIDE8)


def strip_indices(order_ref, tail, width):
    count = order_ref.shape[1]
    return jnp.where(tail, order_ref[:, count - width :], order_ref[:, :width])


def strip_places(jitter_ref, tail, width, unit):
    count = jitter_ref.shape[2]

    def part(component):
        row = jitter_ref[component]
        return jnp.where(tail, row[:, count - width :], row[:, :width])

    start = jnp.where(tail, count - width, 0)
    index = (lax.broadcasted_iota(jnp.int32, (1, width), 1) + start).astype(F32)
    along = (index + part(0)) * (unit / count)
    return along, part(1) * unit, part(2) * unit


def stack_rows(rows, total):
    width = rows[0].shape[1]
    sublane = lax.broadcasted_iota(jnp.int32, (total, width), 0)
    result = jnp.zeros((total, width), F32)
    for position, row in enumerate(rows):
        result = jnp.where(sublane == position, row, result)
    return result


def fill_selector(index, wide_ref, fine_ref):
    count, width = wide_ref.shape
    for first in range(0, count, ROWS):
        row = lax.broadcasted_iota(jnp.int32, (ROWS, width), 0) + first
        hit = jnp.where(row == index, 1.0, 0.0)
        wide_ref[pl.ds(first, ROWS), :] = hit.astype(BF16)
        fine_ref[pl.ds(first, ROWS), :] = hit.astype(FINE8)


def cross_kernel(unit, order_hbm, jitter_hbm, x_ref, upper_ref, lower_ref, high_ref, low_ref, *refs):
    sel_ref, sel8_ref, x_buf, sems, order_ref, jitter_ref, small_sems = refs
    count, points = high_ref.shape
    width = upper_ref.shape[1]
    pieces = points // LANES
    parts = x_buf.shape[0]
    rows = count // parts
    tail = (lax.axis_index("leaf") & 1) == 1

    def copies(part):
        here = pl.ds(part * rows, rows)
        return [
            pltpu.make_async_copy(x_ref.at[here, piece, :], x_buf.at[part, piece], sems.at[part, piece])
            for piece in range(pieces)
        ]

    def split(part):
        here = pl.ds(pl.multiple_of(part * rows, rows), rows)
        for piece in range(pieces):
            value = x_buf[part, piece]
            high = value.astype(BF16)
            lanes = pl.ds(piece * LANES, LANES)
            high_ref[here, lanes] = high
            low_ref[here, lanes], low_ref[here, pl.ds(points + piece * LANES, LANES)] = remainders(value, high)

    def pick(first, size):
        here = pl.ds(first, size)
        return dot(high_ref[here, :], sel_ref[...]) + dot(low_ref[here, :points], sel8_ref[...]) * (1.0 / LO_UP)

    small = [
        pltpu.make_async_copy(order_hbm, order_ref, small_sems.at[0]),
        pltpu.make_async_copy(jitter_hbm, jitter_ref, small_sems.at[1]),
    ]
    for copy in small:
        copy.start()
    for part in range(parts):
        for copy in copies(part):
            copy.start()
    for copy in small:
        copy.wait()
    half = count // 2
    fill_selector(strip_indices(order_ref, tail, width), sel_ref, sel8_ref)
    upper_ref[half:, :] = stack_rows(strip_places(jitter_ref, tail, width, unit), 8)

    def early(part, carry):
        for copy in copies(part):
            copy.wait()
        split(part)
        return carry

    lax.fori_loop(0, parts // 2, early, 0)
    for part in range(parts // 2, parts):
        for copy in copies(part):
            copy.wait()
    for part in range(parts // 2, parts):
        split(part)
    upper_ref[:half, :] = pick(0, half)
    lower_ref[...] = pick(half, half)


def places_kernel(unit, order_ref, jitter_ref, base_ref, spread_ref, base16_ref, base8_ref, far_ref, packed_ref):
    step = pl.program_id(0)
    points = order_ref.shape[1]
    rank = base_ref.shape[0]
    rows = base16_ref.shape[0]

    @pl.when(step == 0)
    def _():
        high, low = split2(base_ref[...])
        packed_ref[0:rank, :] = high
        packed_ref[rank : 2 * rank, :] = low
        index = lax.broadcasted_iota(jnp.int32, (1, points), 1).astype(F32)
        coords = [(index + jitter_ref[0]) * (unit / points), jitter_ref[1] * unit, jitter_ref[2] * unit]
        rest = coords
        pieces = []
        for _ in range(3):
            rounded = [r.astype(BF16).astype(F32) for r in rest]
            pieces.extend(rounded)
            rest = [r - q for r, q in zip(rest, rounded)]
        packed_ref[2 * rank : 2 * rank + 16, :] = stack_rows(pieces, 16).astype(BF16)
        packed_ref[2 * rank + 16 :, :] = jnp.zeros((2 * LANES - 2 * rank - 16, points), BF16)
        far_ref[0:rank, :] = high
        far_ref[rank : 2 * rank, :] = high
        far_ref[2 * rank : 3 * rank, :] = low
        far_ref[3 * rank :, :] = low

    row = lax.broadcasted_iota(jnp.int32, (rows, points), 0) + step * rows
    hit = jnp.where(row == order_ref[...], 1.0, 0.0).astype(BF16)
    moved = lax.dot_general(hit, packed_ref[...], (((1,), (1,)), ((), ())), preferred_element_type=F32)
    both = moved[:, :LANES]
    swap = pltpu.roll(both, LANES // 2, 1)
    left = lax.broadcasted_iota(jnp.int32, (rows, LANES), 1) < LANES // 2
    high = jnp.where(left, both, swap)
    low = jnp.where(left, swap, both)
    base16_ref[:, :LANES] = high.astype(BF16)
    base16_ref[:, LANES:] = low.astype(BF16)
    base8_ref[...] = (high * BASE_UP).astype(FINE8)
    place = moved[:, LANES:]
    place = place + pltpu.roll(place, LANES - 3, 1) + pltpu.roll(place, LANES - 6, 1)
    for component in range(3):
        spread_ref[component] = jnp.broadcast_to(place[:, component : component + 1], (rows, LANES))


def twice(block):
    wide = jnp.concatenate([block, block], axis=1)
    left = lax.broadcasted_iota(jnp.int32, wide.shape, 1) < block.shape[1]
    return jnp.concatenate([jnp.where(left, wide, 0.0), jnp.where(left, 0.0, wide)], axis=0)


def matrices_kernel(leaf_levels, transfer_ref, coupling_ref, lift_ref, couple_ref, last_ref):
    levels = transfer_ref.shape[0]
    leaf = lax.axis_index("leaf")
    sub = lax.axis_index("sub")
    down = None
    span = 2 * transfer_ref.shape[2]
    upper = levels - 1
    for level in range(levels):
        bit = leaf >> level & 1 if level < leaf_levels else sub >> (level - leaf_levels) & 1
        right = bit == 1
        first, second = transfer_ref[level, 0], transfer_ref[level, 1]
        own = jnp.where(right, second, first)
        other = jnp.where(right, first, second)
        couple = jnp.where(right, coupling_ref[level, 1], coupling_ref[level, 0]).T
        if down is not None:
            couple = jnp.dot(couple, down, precision=PRECISE, preferred_element_type=F32)
        high, low = split2(twice(couple))
        if level == 0:
            step_high, step_low = split2(twice(own.T))
            for position, part in enumerate((high, step_high, high, step_high, low, step_low)):
                last_ref[pl.ds(position * span, span), :] = part
        else:
            couple_ref[pl.ds((level - 1) * span, span), :] = high
            couple_ref[pl.ds((upper + level - 1) * span, span), :] = high
            couple_ref[pl.ds((2 * upper + level - 1) * span, span), :] = low
        if level < levels - 1:
            if level > 0:
                down = own.T if down is None else jnp.dot(own.T, down, precision=PRECISE, preferred_element_type=F32)
            own_high, own_low = split2(twice(own))
            other_high, other_low = split2(twice(other))
            for position, part in enumerate((own_high, other_high, own_high, other_high, own_low, other_low)):
                lift_ref[level, pl.ds(position * span, span), :] = part


def core_kernel(unit, order_ref, jitter_ref, base16_ref, base8_ref, high_ref, low_ref, strip_ref, sel_ref, sel8_ref):
    count, points = high_ref.shape
    width = sel_ref.shape[1]
    tail = (lax.axis_index("leaf") & 1) == 0
    fill_selector(strip_indices(order_ref, tail, width), sel_ref, sel8_ref)
    strip_ref[count:, :width] = stack_rows(strip_places(jitter_ref, tail, width, unit), 8)
    strip_ref[count // 2 :, width:] = jnp.zeros((count // 2 + 8, LANES), F32)
    high = high_ref[...]
    low = low_ref[:, :points]
    moment = dot(high, base16_ref[...])
    moment = moment[:, :LANES] + moment[:, LANES:] + dot(low, base8_ref[...]) * MOMENT_DOWN
    half = GROUP // 2
    left = lax.broadcasted_iota(jnp.int32, (half, LANES), 1) < LANES // 2
    for group in range(count // GROUP):
        first = group * GROUP
        packed = jnp.where(left, moment[first : first + half], moment[first + half : first + GROUP])
        strip_ref[group * half : (group + 1) * half, width:] = packed
    strip_ref[:count, :width] = dot(high, sel_ref[...]) + dot(low, sel8_ref[...]) * (1.0 / LO_UP)


def split_product(values, matrix):
    parts = [split2(value) for value in values]
    stacked = [p[0] for p in parts] + [p[1] for p in parts] + [p[0] for p in parts]
    return dot(jnp.concatenate(stacked, axis=1), matrix)


def lift_kernel(level, own_ref, other_ref, matrix_ref, out_ref):
    out_ref[...] = split_product([own_ref[...], other_ref[...]], matrix_ref[level])


def first_lift_kernel(own_ref, other_ref, matrix_ref, out_ref):
    rows = out_ref.shape[0]
    width = own_ref.shape[1] - LANES
    here = pl.ds(pl.multiple_of((lax.axis_index("leaf") & 1) * rows, rows), rows)
    out_ref[...] = split_product([own_ref[here, width:], other_ref[here, width:]], matrix_ref[0])


def collect_kernel(*refs):
    sib_refs, couple_ref, out_ref = refs[:-2], refs[-2], refs[-1]
    out_ref[...] = split_product([ref[...] for ref in sib_refs], couple_ref[...])


def target_places(jitter_ref, unit, place_ref):
    points = jitter_ref.shape[2]
    index = lax.broadcasted_iota(jnp.int32, (1, points), 1).astype(F32)
    rows = [(index + jitter_ref[0]) * (unit / points), jitter_ref[1] * unit, jitter_ref[2] * unit]
    place_ref[...] = stack_rows(rows, 8)


def fill_weights(unit, place_ref, spread_ref, high_ref, fine_ref, columns, sources, looped=False):
    root = unit * math.sqrt(DELTA_SQ)

    def one(block):
        here = pl.ds(block, ROWS)
        for part in range(TILE // LANES):
            lanes = pl.ds(part * LANES, LANES)
            square = root * root
            for component in range(3):
                there = place_ref[component : component + 1, pl.ds(columns + part * LANES, LANES)]
                gap = spread_ref[component, here, :] - there
                square = gap * gap + square
            store_weight(square, high_ref, fine_ref, here, pl.ds(sources + block, ROWS), lanes)

    if looped:

        def run(index, carry):
            one(pl.multiple_of(index * ROWS, ROWS))
            return carry

        lax.fori_loop(0, sources // ROWS, run, 0)
    else:
        for block in range(0, sources, ROWS):
            one(block)


def own_kernel(unit, chunk, jitter_ref, spread_ref, high_ref, low_ref, *refs):
    out_ref, ha, wa, place_ref, hb, wb = refs[-6:]
    chunks = out_ref.shape[0]
    points = high_ref.shape[1]
    target_places(jitter_ref, unit, place_ref)

    def fill(tile, high, fine, looped=False):
        fill_weights(unit, place_ref, spread_ref, high, fine, tile * TILE, points, looped)

    def product(tile, high, fine):
        value = dot(high_ref[...], high[...]) + dot(low_ref[...], fine[...]) * NEAR_DOWN
        out_ref[chunk, :, tile * TILE : (tile + 1) * TILE] = value

    if chunk == 0:
        fill(0, ha, wa, True)
    fill(2 * chunk + 1, hb, wb)
    product(0, ha, wa)
    if chunk + 1 < chunks:
        fill(2 * chunk + 2, ha, wa)
    product(1, hb, wb)


def store_weight(square, high_ref, fine_ref, here, there, lanes):
    weight = lax.rsqrt(square)
    high = weight.astype(BF16)
    high_ref[here, lanes] = high
    fine_ref[here, lanes] = (high * BF16(W_UP)).astype(FINE8)
    rest = (weight - high.astype(F32)).astype(BF16)
    fine_ref[there, lanes] = (rest * BF16(W_LO_UP)).astype(FINE8)


def place_strip(spread_ref, across, shift):
    for component in range(3):
        column = across[:, component : component + 1]
        if component == 0:
            column = column + shift
        spread_ref[component] = jnp.broadcast_to(column, spread_ref.shape[1:])


def take_strip(left_ref, low_ref, rows, value):
    width = value.shape[1]
    high = value.astype(BF16)
    left_ref[rows, :width] = high
    low_ref[rows, :width], low_ref[rows, width:] = remainders(value, high)


def core_shift(unit):
    odd = (lax.axis_index("leaf") & 1) == 1
    return jnp.where(odd, -unit, unit)


def middle_kernel(unit, jitter_ref, core_ref, near_ref, out_ref, left_ref, low_ref, spread_ref, place_ref, ha, wa, hb, wb):
    chunks, count, _ = near_ref.shape
    width = left_ref.shape[1]
    target_places(jitter_ref, unit, place_ref)
    place_strip(spread_ref, core_ref[count:, :width].T, core_shift(unit))

    def fill(tile, high, fine):
        fill_weights(unit, place_ref, spread_ref, high, fine, pl.multiple_of(tile * TILE, TILE), width)

    fill_weights(unit, place_ref, spread_ref, ha, wa, 0, width, True)
    take_strip(left_ref, low_ref, pl.ds(0, count), core_ref[:count, :width])

    def product(pair, tile, h, w):
        lanes = slice(tile * TILE, (tile + 1) * TILE)
        out_ref[pair, :, lanes] = (
            near_ref[pair, :, lanes] + dot(left_ref[...], h[...]) + dot(low_ref[...], w[...]) * NEAR_DOWN
        )

    def run(pair, carry):
        fill(2 * pair + 1, hb, wb)
        product(pair, 0, ha, wa)
        fill(jnp.minimum(2 * pair + 2, 2 * chunks - 1), ha, wa)
        product(pair, 1, hb, wb)
        return carry

    lax.fori_loop(0, chunks, run, 0)


def final_kernel(unit, jitter_ref, core_ref, upper_ref, lower_ref, mine_ref, other_ref, last_ref, far_ref, near_ref, *refs):
    out_ref, left_ref, low_ref, spread_ref, place_ref, ha, wa, hb, wb, stage_ref, sems = refs
    chunks, count, _ = near_ref.shape
    width = upper_ref.shape[1]

    def fill(tile, high, fine):
        columns = pl.multiple_of(tile * TILE, TILE)
        fill_weights(unit, place_ref, spread_ref, high, fine, columns, width)
        high[width:, :] = far_ref[:, pl.ds(columns, TILE)]

    target_places(jitter_ref, unit, place_ref)
    place_strip(spread_ref, upper_ref[count // 2 :, :].T, -core_shift(unit))
    fill(0, ha, wa)
    take_strip(left_ref.at[:, pl.ds(0, width)], low_ref, pl.ds(0, count // 2), upper_ref[: count // 2, :])
    take_strip(left_ref.at[:, pl.ds(0, width)], low_ref, pl.ds(count // 2, count // 2), lower_ref[...])
    even = (lax.axis_index("leaf") & 1) == 0
    mine, other = mine_ref[...], other_ref[...]
    above = jnp.concatenate([jnp.where(even, mine, other), jnp.where(even, other, mine)], axis=0)
    expansion = split_product([core_ref[: count // 2, width:], above], last_ref[...])
    high = expansion.astype(BF16).astype(F32)
    low = pltpu.roll(expansion - high, LANES // 2, 1)
    half = GROUP // 2
    is_left = lax.broadcasted_iota(jnp.int32, (half, LANES), 1) < LANES // 2
    for block in range(count // GROUP):
        h = high[block * half : (block + 1) * half]
        l = low[block * half : (block + 1) * half]
        first = pl.ds(block * GROUP, half)
        second = pl.ds(block * GROUP + half, half)
        left_ref[first, width : width + LANES] = jnp.where(is_left, h, l).astype(BF16)
        left_ref[second, width : width + LANES] = jnp.where(is_left, l, h).astype(BF16)
        left_ref[first, width + LANES :] = jnp.where(is_left, h, 0.0).astype(BF16)
        left_ref[second, width + LANES :] = jnp.where(is_left, 0.0, h).astype(BF16)

    parts_per_tile = TILE // LANES

    def copy(pair, tile):
        slot = 2 * (pair % 2) + tile
        lanes = pl.ds((2 * pair + tile) * parts_per_tile, parts_per_tile)
        return pltpu.make_async_copy(
            stage_ref.at[slot].reshape(count, parts_per_tile, LANES), out_ref.at[:, lanes, :], sems.at[slot]
        )

    def product(pair, tile, h, w):
        lanes = slice(tile * TILE, (tile + 1) * TILE)
        value = near_ref[pair, :, lanes] + dot(left_ref[...], h[...]) + dot(low_ref[...], w[...]) * NEAR_DOWN
        for part in range(parts_per_tile):
            stage_ref[2 * (pair % 2) + tile, pl.ds(part, count, stride=parts_per_tile), :] = value[
                :, part * LANES : (part + 1) * LANES
            ]

    def run(pair, carry):
        @pl.when(pair >= 2)
        def _():
            copy(pair - 2, 0).wait()
            copy(pair - 2, 1).wait()

        fill(2 * pair + 1, hb, wb)
        product(pair, 0, ha, wa)
        copy(pair, 0).start()
        fill(jnp.minimum(2 * pair + 2, 2 * chunks - 1), ha, wa)
        product(pair, 1, hb, wb)
        copy(pair, 1).start()
        return carry

    lax.fori_loop(0, chunks, run, 0)
    for pair in range(chunks - 2, chunks):
        copy(pair, 0).wait()
        copy(pair, 1).wait()


def cost(flops, moved):
    return pl.CostEstimate(flops=int(flops), bytes_accessed=int(moved), transcendentals=0)


def whole(array):
    rank = len(array.shape)
    return pl.BlockSpec(array.shape, lambda *_: (0,) * rank)


def shape(dims, dtype=F32):
    return jax.ShapeDtypeStruct(dims, dtype)


def body(charges, ordering, jitter, leaf_bases, transfer, coupling):
    points = charges.shape[4]
    count = charges.shape[0] * charges.shape[1]
    width = points // 4
    rank = leaf_bases.shape[2]
    unit = math.sqrt(points)
    leaf_count = lax.axis_size("leaf")
    sub_count = lax.axis_size("sub")
    leaf_levels = leaf_count.bit_length() - 1
    sub_levels = sub_count.bit_length() - 1
    levels = leaf_levels + sub_levels
    half = count // 2
    pieces = points // LANES
    x = charges.reshape(count, pieces, LANES)
    order = ordering.reshape(1, points)
    offsets = jitter.reshape(3, 1, points)
    base = leaf_bases.reshape(rank, points)
    params = lambda mib: pltpu.CompilerParams(vmem_limit_bytes=mib << 20)
    vmem = pl.BlockSpec(memory_space=pltpu.VMEM)

    in_hbm = lambda array: pltpu.with_memory_space_constraint(array, pltpu.HBM)
    parts = 4
    upper, lower, high, low = pl.pallas_call(
        functools.partial(cross_kernel, unit),
        in_specs=[pl.BlockSpec(memory_space=pltpu.HBM)] * 3,
        out_specs=[vmem] * 4,
        out_shape=[
            shape((half + 8, width)),
            shape((half, width)),
            shape((count, points), BF16),
            shape((count, 2 * points), WIDE8),
        ],
        scratch_shapes=[
            pltpu.VMEM((points, width), BF16),
            pltpu.VMEM((points, width), FINE8),
            pltpu.VMEM((parts, pieces, count // parts, LANES), F32),
            pltpu.SemaphoreType.DMA((parts, pieces)),
            pltpu.VMEM((1, points), jnp.int32),
            pltpu.VMEM((3, 1, points), F32),
            pltpu.SemaphoreType.DMA((2,)),
        ],
        compiler_params=params(20),
        cost_estimate=cost(3 * count * points * width, 16 * count * points),
        name="cross",
    )(in_hbm(order), in_hbm(offsets), in_hbm(x))
    last = leaf_count - 1
    middle = leaf_count // 2
    up_pairs = [(i, i + 1) for i in range(1, last, 2)]
    direct = up_pairs + [(b, a) for a, b in up_pairs]
    ends = (0, middle - 1, middle, last)
    to_relay = [(middle - 1, last), (middle, 0)] + [(i, i) for i in range(leaf_count) if i not in ends]
    relayed = [p for p in direct if p[0] not in ends] + [(last, middle), (0, middle - 1)]
    if leaf_count < 4:
        to_relay, relayed = [], []
    upper_in = lax.ppermute(upper, "leaf", direct)
    relay = lax.ppermute(lower, "leaf", to_relay)

    spread, base16, base8, far = pl.pallas_call(
        functools.partial(places_kernel, unit),
        grid=(points // GROUP,),
        in_specs=[whole(order), whole(offsets), whole(base)],
        out_specs=[
            pl.BlockSpec((3, GROUP, LANES), lambda i: (0, i, 0)),
            pl.BlockSpec((GROUP, 2 * LANES), lambda i: (i, 0)),
            pl.BlockSpec((GROUP, LANES), lambda i: (i, 0)),
            pl.BlockSpec((4 * rank, points), lambda i: (0, 0)),
        ],
        out_shape=[
            shape((3, points, LANES)),
            shape((points, 2 * LANES), BF16),
            shape((points, LANES), FINE8),
            shape((4 * rank, points), BF16),
        ],
        scratch_shapes=[pltpu.VMEM((2 * LANES, points), BF16)],
        compiler_params=params(16),
        cost_estimate=cost(2 * points * points * 256, 5 * points * 1024),
        name="places",
    )(order, offsets, base)

    core = pl.pallas_call(
        functools.partial(core_kernel, unit),
        in_specs=[vmem] * 6,
        out_specs=vmem,
        out_shape=shape((count + 8, width + LANES)),
        scratch_shapes=[pltpu.VMEM((points, width), BF16), pltpu.VMEM((points, width), FINE8)],
        compiler_params=params(16),
        cost_estimate=cost(3 * count * points * (width + 256), 6 * count * points),
        name="core",
    )(order, offsets, base16, base8, high, low)
    core_in = lax.ppermute(core, "leaf", [(i, i ^ 1) for i in range(leaf_count)])

    lift, couple, last_matrix = pl.pallas_call(
        functools.partial(matrices_kernel, leaf_levels),
        in_specs=[vmem] * 2,
        out_specs=[vmem] * 3,
        out_shape=[
            shape((levels - 1, 12 * rank, 2 * rank), BF16),
            shape((6 * (levels - 1) * rank, 2 * rank), BF16),
            shape((12 * rank, 2 * rank), BF16),
        ],
        compiler_params=params(8),
        cost_estimate=cost(1e6, 1e6),
        name="matrices",
    )(transfer, coupling)

    chunks = points // (2 * TILE)

    def own(chunk, *carried):
        return pl.pallas_call(
            functools.partial(own_kernel, unit, chunk),
            in_specs=[vmem] * 4 + [pl.BlockSpec(memory_space=pl.ANY)] * len(carried),
            out_specs=[vmem] * 3,
            out_shape=[shape((chunks, count, 2 * TILE)), shape((points, TILE), BF16), shape((2 * points, TILE), FINE8)],
            scratch_shapes=[
                pltpu.VMEM((8, points), F32),
                pltpu.VMEM((points, TILE), BF16),
                pltpu.VMEM((2 * points, TILE), FINE8),
            ],
            input_output_aliases={4 + i: i for i in range(len(carried))},
            compiler_params=params(8),
            cost_estimate=cost(8 * count * points * TILE, 10 * count * points),
        )(offsets, spread, high, low, *carried)

    quarter = half // 2

    def small(kernel, operands):
        return pl.pallas_call(
            kernel,
            in_specs=[vmem] * len(operands),
            out_specs=vmem,
            out_shape=shape((quarter, LANES)),
            compiler_params=params(4),
            cost_estimate=cost(2 * quarter * 768 * 128, 3 * quarter * 512),
        )(*operands)

    carried = own(0)
    siblings = []
    current = small(first_lift_kernel, (core, core_in, lift))
    for level in range(1, levels):
        if level > 1:
            kernel = functools.partial(lift_kernel, level - 1)
            current = small(kernel, (current, siblings[-1], lift))
        axis, bit = ("leaf", level) if level < leaf_levels else ("sub", level - leaf_levels)
        pairs = [(i, i ^ 1 << bit) for i in range(lax.axis_size(axis))]
        siblings.append(lax.ppermute(current, axis, pairs))
        if level == 1:
            lower_in = lax.ppermute(relay, "leaf", relayed)
        if level < chunks:
            carried = own(level, *carried)
    for chunk in range(levels, chunks):
        carried = own(chunk, *carried)
    mine = small(collect_kernel, (*siblings, couple))
    other = lax.ppermute(mine, "leaf", [(i, i ^ 1) for i in range(leaf_count)])

    def strip_scratch(extra):
        tall = width + extra
        return [
            pltpu.VMEM((count, tall), BF16),
            pltpu.VMEM((count, 2 * width), WIDE8),
            pltpu.VMEM((3, width, LANES), F32),
            pltpu.VMEM((8, points), F32),
        ] + [pltpu.VMEM((tall, TILE), BF16), pltpu.VMEM((2 * width, TILE), FINE8)] * 2

    near = pl.pallas_call(
        functools.partial(middle_kernel, unit),
        in_specs=[vmem] * 3,
        out_specs=vmem,
        out_shape=shape((chunks, count, 2 * TILE)),
        scratch_shapes=strip_scratch(0),
        input_output_aliases={2: 0},
        compiler_params=params(12),
        cost_estimate=cost(4 * count * points * width, 8 * count * points),
        name="middle",
    )(offsets, core_in, carried[0])

    out = pl.pallas_call(
        functools.partial(final_kernel, unit),
        in_specs=[vmem] * 9,
        out_specs=pl.BlockSpec(memory_space=pl.ANY),
        out_shape=shape((count, pieces, LANES)),
        scratch_shapes=strip_scratch(4 * rank)
        + [pltpu.VMEM((4, count * TILE // LANES, LANES), F32), pltpu.SemaphoreType.DMA((4,))],
        compiler_params=params(20),
        cost_estimate=cost(4 * count * points * width, 8 * count * points),
        name="final",
    )(offsets, core_in, upper_in, lower_in, mine, other, last_matrix, far, near)
    return out.reshape(charges.shape)


def solution(mesh):
    in_specs = (
        P(None, None, "sub", "leaf", None),
        P("sub", "leaf", None),
        P(None, "sub", "leaf", None),
        P("sub", "leaf", None, None),
        P(),
        P(),
    )
    out_specs = P(None, None, "sub", "leaf", None)

    return jax.shard_map(body, mesh=mesh, in_specs=in_specs, out_specs=out_specs, check_vma=False)
```
